256 devices in a mesh: ctx: 16 (over y_hi, z), head: 16 (over y_lo, x, core).
Axes of the slice: x: 4, y: 4 (y_hi: 2, y_lo: 2; y = y_hi * 2 + y_lo), z: 8, core: 2. Of those that a mesh axis runs over, the one named last changes fastest.
Arguments:
- q_nope: bfloat16 [4096, 16384], P('ctx', 'head'), may hold values from -4 to 4
- q_rope: bfloat16 [4096, 8192], P('ctx', 'head'), may hold values from -8 to 8
- kv_latent: bfloat16 [4096, 576], P(('ctx', 'head')), may hold values from -6 to 6
- half_order: int32 [32], replicated, may hold values from 0 to 31, as said below
- w_uk: bfloat16 [128, 128, 512], P('head'), may hold values from -0.5 to 0.5
- w_uv: bfloat16 [128, 512, 128], P('head'), may hold values from -1.5 to 1.5
Outputs:
- attended: bfloat16 [4096, 16384], P('ctx', 'head')
The draws below stay inside these ranges and needn't reach their ends.
Inputs may be any that keep to these rules, and one draw needn't show every extreme that they name: `half_order`: a permutation of 0 to 31.
All inputs are finite; a program needn't handle non-finite values.
Results may differ from the reference program's by a relative error of at most 0.0085.
Values may be sent and summed in bfloat16 or wider, within the bound.
No kernel may reach another device: no remote copies, remote signals or barrier semaphores. Data moves between devices by JAX's collectives and lax.ppermute only.
A program may use at most 64 MiB of HBM per device.

```python
import jax
import jax.numpy as jnp
from jax import lax

HEADS = 128
LATENT = 512
ROPE = 64
NOPE = 128
VDIM = 128
TOKENS = 4096
HALVES = 32


def order_of(key):
    return jax.random.permutation(jax.random.fold_in(key, 11), HALVES).astype(jnp.int32)


def draw_half_order(key, part):
    return order_of(key)


def draw_q_rope(key, part):
    inner_key = jax.random.fold_in(key, 31)
    base = jnp.clip(jax.random.normal(inner_key, (TOKENS, HEADS, ROPE), jnp.float32), -4.0, 4.0)
    return base.reshape(TOKENS, HEADS * ROPE).astype(jnp.bfloat16)


def draw_kv_latent(key, part):
    inner_key = jax.random.fold_in(key, 41)
    base = jnp.clip(jax.random.normal(inner_key, (TOKENS, LATENT + ROPE), jnp.float32), -4.0, 4.0)
    return base.astype(jnp.bfloat16)


def levels(own_key, extent, shards, smallest, top_value):
    def one(dim, parts):
        draws = jax.random.uniform(jax.random.fold_in(jax.random.fold_in(own_key, 6), dim), (parts,), jnp.float32, smallest / len(shards), top_value / len(shards))
        return jnp.repeat(jnp.exp(draws), extent[dim] // parts).reshape((-1,) + (1,) * (len(extent) - dim - 1))

    loudness = one(*shards[0])
    for cut in shards[1:]:
        loudness = loudness * one(*cut)
    return loudness


def noise(rng, dims, deviation, most, cuts=(), kind=jnp.bfloat16):
    drawn = deviation * jax.random.normal(rng, dims, jnp.float32)
    if cuts:
        drawn = drawn * levels(rng, dims, cuts, -0.22, 0.18)
    return jnp.clip(drawn, -most, most).astype(kind)


def setup_inputs(seed: int = 0) -> dict:
    arg_keys = jax.random.split(jax.random.key(seed), 7)
    return {
        "q_nope": noise(arg_keys[0], (TOKENS, HEADS * NOPE), 1.0, 4.0, ((0, 16), (1, 16))),
        "q_rope": draw_q_rope(jax.random.fold_in(arg_keys[6], 71), 0),
        "kv_latent": draw_kv_latent(jax.random.fold_in(arg_keys[6], 71), 0),
        "half_order": draw_half_order(jax.random.fold_in(arg_keys[6], 71), 0),
        "w_uk": noise(arg_keys[4], (HEADS, NOPE, LATENT), NOPE ** -0.5, 0.5, ((0, 16),)),
        "w_uv": noise(arg_keys[5], (HEADS, LATENT, VDIM), (LATENT // 32) ** -0.5, 1.5, ((0, 16),)),
    }


def reference(q_nope, q_rope, kv_latent, half_order, w_uk, w_uv):
    head_count, nope_width, latent_width = w_uk.shape
    value_width = w_uv.shape[2]
    token_count = q_nope.shape[0]
    rope_width = q_rope.shape[1] // head_count
    half_rows = token_count // half_order.shape[0]
    index_rows = jnp.arange(token_count, dtype=jnp.int32)
    position = half_order[index_rows // half_rows] * half_rows + index_rows % half_rows
    visible = position[None, :] <= position[:, None]
    key_latent = kv_latent[:, :latent_width].astype(jnp.float32)
    key_rope = kv_latent[:, latent_width:].astype(jnp.float32)
    score_scale = (nope_width + rope_width) ** -0.5
    queries = q_nope.reshape(token_count, head_count, nope_width).transpose(1, 0, 2)
    query_rope = q_rope.reshape(token_count, head_count, rope_width).transpose(1, 0, 2)

    def one_head(operands):
        query_head, rope_head, key_weight, value_weight = operands
        query_latent = jnp.dot(query_head.astype(jnp.float32), key_weight.astype(jnp.float32)).astype(jnp.bfloat16)
        scores = jnp.dot(query_latent.astype(jnp.float32), key_latent.T) + jnp.dot(rope_head.astype(jnp.float32), key_rope.T)
        scores = scores * score_scale
        masked = jnp.where(visible, scores, -1e30)
        row_max = jnp.max(masked, axis=1, keepdims=True)
        weights = jnp.where(visible, jnp.exp(jnp.minimum(scores - row_max, 0.0)), 0.0)
        weight_sum = jnp.sum(weights, axis=1, keepdims=True)
        summed = jnp.dot(weights.astype(jnp.bfloat16).astype(jnp.float32), key_latent)
        out_latent = (summed / weight_sum).astype(jnp.bfloat16)
        return jnp.dot(out_latent.astype(jnp.float32), value_weight.astype(jnp.float32)).astype(jnp.bfloat16)

    outputs = lax.map(one_head, (queries, query_rope, w_uk, w_uv))
    return outputs.transpose(1, 0, 2).reshape(token_count, head_count * value_width)
```

```python
import functools

import jax
import jax.numpy as jnp
import numpy as np
from jax import lax
from jax.experimental import pallas as pl
from jax.experimental.pallas import tpu as pltpu
from jax.sharding import PartitionSpec as P


HEADS = 8
ROWS = 256
NOPE = 128
LATENT = 512
ROPE = 64
PIECE = 256
SCALE = (NOPE + ROPE) ** -0.5 * 1.4426950408889634
LOW = -1e30
NT = (((1,), (1,)), ((), ()))
NN = (((1,), (0,)), ((), ()))
CALLS = ((0, 1, 3, 2),)
HEAD_TILE = 2
NZ, NY, NX = 8, 4, 4


def index_of(z, y, x, c):
    ctx = (y // 2) * NZ + z
    head = ((y % 2) * NX + x) * 2 + c
    return ctx * 16 + head


def shift(value, dz=0, dy=0, dx=0, dc=0):
    pairs = [
        (
            index_of(z, y, x, c),
            index_of((z + dz) % NZ, (y + dy) % NY, (x + dx) % NX, (c + dc) % 2),
        )
        for z in range(NZ)
        for y in range(NY)
        for x in range(NX)
        for c in range(2)
    ]
    return lax.ppermute(value, ("ctx", "head"), pairs)


def key_positions(half_order, chunk):
    ctx, head = lax.axis_index("ctx"), lax.axis_index("head")
    z, y = ctx % NZ, (ctx // NZ) * 2 + head // 8
    x, c = (head // 2) % NX, head % 2
    axis = np.arange(4)[:, None, None]
    dz = np.arange(8)[None, :, None]
    row = np.arange(8)[None, None, :]
    flat = lambda a: np.broadcast_to(a, (4, 8, 8)).reshape(256)
    dz = np.tile(flat(dz), 4).astype(np.int32)
    same = np.full(256, chunk)
    dy = np.concatenate([flat(axis), same, flat(axis), same]).astype(np.int32)
    dx = np.concatenate([same, flat(axis), same, flat(axis)]).astype(np.int32)
    dc = np.repeat(np.array([0, 0, 1, 1]), 256).astype(np.int32)
    r = np.tile(np.concatenate([flat(row), flat(row) + 8]), 2).astype(np.int32)
    zs, ys, xs, cs = (z - dz) % NZ, (y - dy) % NY, (x - dx) % NX, (c + dc) % 2
    half = 2 * ((ys // 2) * NZ + zs) + ys % 2
    onehot = half[None, :] == jnp.arange(32, dtype=jnp.int32)[:, None]
    block = jnp.sum(jnp.where(onehot, half_order[:, None], 0), axis=0)
    return (block * 128 + (xs * 2 + cs) * 16 + r)[None, :]


def query_positions(half_order):
    ctx = lax.axis_index("ctx")
    block = lax.dynamic_slice(half_order, (ctx * 2,), (2,))
    pos = (block[:, None] * 128 + jnp.arange(128, dtype=jnp.int32)[None, :]).reshape(ROWS, 1)
    return jnp.broadcast_to(pos, (ROWS, 128))


def attend(first, last, blocks, *refs):
    f32, bf16 = jnp.float32, jnp.bfloat16
    refs = list(refs)
    take = lambda n: [refs.pop(0) for _ in range(n)]
    qpos, qn, qr, wuk = take(4)
    kpos = take(blocks)
    pieces = [take(4) for _ in range(blocks)]
    wuv = take(1)[0] if last else None
    state_in = None if first else take(3)
    if last:
        out = take(1)[0]
    else:
        acc, mref, lref = take(3)
    qx, kv, kn, kr, sbuf = take(5)
    if last:
        acc, mref, lref = take(3) if first else state_in
    elif not first:
        pass
    size = 4 * PIECE
    tiles = HEADS // HEAD_TILE
    zq = jnp.zeros((ROWS, 64), bf16)
    zk = jnp.zeros((PIECE, 64), bf16)
    for h in range(HEADS):
        qx[h * ROWS : (h + 1) * ROWS, 0:128] = qn[:, h * 128 : (h + 1) * 128]
        qx[h * ROWS : (h + 1) * ROWS, 128:256] = jnp.concatenate(
            [qr[:, h * 64 : (h + 1) * 64], zq], axis=1
        )

    def arrange(kb, slot):
        for j in range(4):
            rows = slice(j * PIECE, (j + 1) * PIECE)
            kv[slot, rows, :] = pieces[kb][j][:, 0:LATENT]
            kr[slot, rows, :] = jnp.concatenate([pieces[kb][j][:, LATENT:], zk], axis=1)

    def expand(slot, a, b):
        kn[slot, :, a * 128 : b * 128] = lax.dot_general(
            kv[slot], wuk[a * 128 : b * 128, :], NT, preferred_element_type=f32
        ).astype(bf16)

    def score(ks, tile, slot, i):
        h = tile * HEAD_TILE + i
        keys = jnp.concatenate([kn[ks, :, h * 128 : (h + 1) * 128], kr[ks]], axis=1)
        sbuf[slot, i * ROWS : (i + 1) * ROWS, :] = lax.dot_general(
            qx[h * ROWS : (h + 1) * ROWS, :], keys, NT, preferred_element_type=f32
        )

    def weigh(kb, ks, tile, slot, i, fresh):
        r0 = (tile * HEAD_TILE + i) * ROWS
        r1 = r0 + ROWS
        a, b = i * ROWS, (i + 1) * ROWS
        qp = qpos[...]
        s = [
            jnp.where(
                kpos[kb][:, c * 128 : (c + 1) * 128] <= qp,
                sbuf[slot, a:b, c * 128 : (c + 1) * 128],
                LOW,
            )
            for c in range(size // 128)
        ]
        top = functools.reduce(jnp.maximum, s)
        top = jnp.max(top, axis=1, keepdims=True)
        if fresh:
            new = jnp.broadcast_to(top, (ROWS, 128))
        else:
            old = mref[r0:r1, :]
            new = jnp.maximum(old, top)
            factor = jnp.exp2((old - new) * SCALE)
        base = new * SCALE
        w = [jnp.exp2(v * SCALE - base) for v in s]
        total = functools.reduce(jnp.add, w)
        mref[r0:r1, :] = new
        lref[r0:r1, :] = total if fresh else lref[r0:r1, :] * factor + total
        wb = jnp.concatenate([v.astype(bf16) for v in w], axis=1)
        product = lax.dot_general(wb, kv[ks], NN, preferred_element_type=f32)
        if fresh:
            acc[r0:r1, :] = product
        else:
            for c in range(LATENT // 128):
                cols = slice(c * 128, (c + 1) * 128)
                acc[r0:r1, cols] = acc[r0:r1, cols] * factor + product[:, cols]

    if not first and not last:
        acc[...] = state_in[0][...]
        mref[...] = state_in[1][...]
        lref[...] = state_in[2][...]
    arrange(0, 0)
    expand(0, 0, HEADS)
    for i in range(HEAD_TILE):
        score(0, 0, 0, i)
    for kb in range(blocks):
        ks, ns = kb % 2, 1 - kb % 2
        for tile in range(tiles):
            slot = tile % 2
            for i in range(HEAD_TILE):
                if tile + 1 < tiles:
                    score(ks, tile + 1, 1 - slot, i)
                elif kb + 1 < blocks:
                    score(ns, 0, 1 - slot, i)
                weigh(kb, ks, tile, slot, i, first and kb == 0)
                if tile == 0 and kb + 1 < blocks:
                    if i == 0:
                        arrange(kb + 1, ns)
                    expand(ns, i * tiles, (i + 1) * tiles)
    if last:
        for h in range(HEADS):
            r0 = h * ROWS
            den = jnp.sum(lref[r0 : r0 + ROWS, :], axis=1, keepdims=True)
            latent = (acc[r0 : r0 + ROWS, :] / den).astype(bf16)
            out[:, h * 128 : (h + 1) * 128] = jnp.dot(
                latent, wuv[h], preferred_element_type=f32
            ).astype(bf16)


def attend_call(first, last, qpos, qn, qr, wuk, kpos, pieces, wuv, state):
    vmem = pltpu.VMEM
    f32, bf16 = jnp.float32, jnp.bfloat16
    blocks = len(pieces)
    args = [qpos, qn, qr, wuk, *kpos, *(p for four in pieces for p in four)]
    if last:
        args.append(wuv)
    alias = {}
    if not first:
        if not last:
            alias = {len(args) + i: i for i in range(3)}
        args.extend(state)
    shapes = [
        jax.ShapeDtypeStruct((HEADS * ROWS, LATENT), f32),
        jax.ShapeDtypeStruct((HEADS * ROWS, 128), f32),
        jax.ShapeDtypeStruct((HEADS * ROWS, 128), f32),
    ]
    size = 4 * PIECE
    scratch = [
        vmem((HEADS * ROWS, 256), bf16),
        vmem((2, size, LATENT), bf16),
        vmem((2, size, HEADS * 128), bf16),
        vmem((2, size, 128), bf16),
        vmem((2, HEAD_TILE * ROWS, size), f32),
    ]
    if last and first:
        scratch += [vmem(s.shape, s.dtype) for s in shapes]
    out_shape = jax.ShapeDtypeStruct((ROWS, HEADS * 128), bf16) if last else shapes
    spec = pl.BlockSpec(memory_space=vmem)
    keys = blocks * size
    return pl.pallas_call(
        functools.partial(attend, first, last, blocks),
        out_shape=out_shape,
        in_specs=[spec] * len(args),
        out_specs=spec if last else [spec] * 3,
        scratch_shapes=scratch,
        input_output_aliases=alias,
        compiler_params=pltpu.CompilerParams(vmem_limit_bytes=44 << 20),
        cost_estimate=pl.CostEstimate(
            flops=2 * HEADS * ROWS * keys * 1024,
            bytes_accessed=8 << 20,
            transcendentals=HEADS * ROWS * keys,
        ),
        name=f"attend_{blocks}",
    )(*args)


def on_device(q_nope, q_rope, kv_latent, half_order, w_uk, w_uv):
    wuk = w_uk.reshape(HEADS * NOPE, LATENT)
    qpos = query_positions(half_order)
    own = kv_latent
    column = [own] + [shift(own, dz=d) for d in range(1, NZ)]
    low = jnp.concatenate([v[:8] for v in column], axis=0)
    high = jnp.concatenate([v[8:] for v in column], axis=0)
    plane_a = jnp.concatenate([low] + [shift(low, dy=d) for d in range(1, NY)], axis=0)
    plane_b = jnp.concatenate([high] + [shift(high, dx=d) for d in range(1, NX)], axis=0)
    chunks = []
    for d in range(4):
        a = shift(plane_a, dx=d) if d else plane_a
        b = shift(plane_b, dy=d) if d else plane_b
        chunks.append((a, b, shift(a, dc=1), shift(b, dc=1)))
    kpos = [key_positions(half_order, d) for d in range(4)]
    state = None
    for n, group in enumerate(CALLS):
        state = attend_call(
            n == 0,
            n == len(CALLS) - 1,
            qpos,
            q_nope,
            q_rope,
            wuk,
            [kpos[d] for d in group],
            [chunks[d] for d in group],
            w_uv,
            state,
        )
    return state


def solution(mesh):
    return jax.shard_map(
        on_device,
        mesh=mesh,
        in_specs=(
            P("ctx", "head"),
            P("ctx", "head"),
            P(("ctx", "head"), None),
            P(),
            P("head", None, None),
            P("head", None, None),
        ),
        out_specs=P("ctx", "head"),
        check_vma=False,
    )
```

```python
import functools

import jax
import jax.numpy as jnp
import numpy as np
from jax import lax
from jax.experimental import pallas as pl
from jax.experimental.pallas import tpu as pltpu
from jax.sharding import Mesh
from jax.sharding import PartitionSpec as P


HEADS = 8
ROWS = 256
NOPE = 128
LATENT = 512
ROPE = 64
PIECE = 512
SCALE = (NOPE + ROPE) ** -0.5 * 1.4426950408889634
LOW = -1e30
NT = (((1,), (1,)), ((), ()))
NN = (((1,), (0,)), ((), ()))
HEAD_TILE = 2
TILES = HEADS // HEAD_TILE
NY = 4
CALLS = ((0, 1), (2,), (3, 4), (5, 6), (7,))


def ring_step(value):
    pairs = [
        (y * 2 + c, ((y + (1 - 2 * c)) % NY) * 2 + c) for y in range(NY) for c in range(2)
    ]
    return lax.ppermute(value, ("yh", "yl", "c"), pairs)


def exchange(value):
    return lax.ppermute(value, "c", [(0, 1), (1, 0)])


def key_positions(half_order):
    y = lax.axis_index("yh") * 2 + lax.axis_index("yl")
    c = lax.axis_index("c")
    ahead = 1 - 2 * c
    ys = jnp.stack([y, y, y - ahead, y + ahead, y - ahead, y + ahead, y + 2, y + 2]) & 3
    cs = jnp.stack([c, 1 - c, c, 1 - c, 1 - c, c, c, 1 - c])
    table = half_order.reshape(2, 8, 2).transpose(0, 2, 1).reshape(4, 8)
    block = jnp.sum(
        jnp.where((ys[:, None] == jnp.arange(4)[None, :])[:, :, None], table[None], 0), axis=1
    )
    j = np.arange(64)
    inner = jnp.asarray((j // 16) * 32 + j % 16, jnp.int32)
    pos = block[:, :, None] * 128 + inner[None, None, :] + cs[:, None, None] * 16
    return pos.reshape(8, PIECE).astype(jnp.int32)


def query_positions(half_order):
    ctx = lax.axis_index("yh") * 8 + lax.axis_index("z")
    block = lax.dynamic_slice(half_order, (ctx * 2,), (2,))
    pos = (block[:, None] * 128 + jnp.arange(128, dtype=jnp.int32)[None, :]).reshape(ROWS, 1)
    return jnp.broadcast_to(pos, (ROWS, 128))


def pack_queries(qn, qr, qx):
    zeros = jnp.zeros((ROWS, 64), jnp.bfloat16)
    for h in range(HEADS):
        rows = slice(h * ROWS, (h + 1) * ROWS)
        qx[rows, 0:128] = qn[:, h * 128 : (h + 1) * 128]
        qx[rows, 128:256] = jnp.concatenate([qr[:, h * 64 : (h + 1) * 64], zeros], axis=1)


def attend(first, last, ids, *refs):
    f32, bf16 = jnp.float32, jnp.bfloat16
    refs = list(refs)
    take = lambda n: [refs.pop(0) for _ in range(n)]
    qpos, kpos, qx, wuk = take(4)
    pieces = take(len(ids))
    wuv = take(1)[0] if last else None
    state = None if first else take(3)
    if last:
        out = take(1)[0]
        acc, mref, lref = state
    else:
        acc, mref, lref = take(3)
    kv, kp, kn, kr, sbuf = take(5)
    zk = jnp.zeros((PIECE, 64), bf16)
    blocks = len(ids)

    def expand(a, b):
        def go(slot):
            kn[:, a * 128 : b * 128] = lax.dot_general(
                kv[slot], wuk[a * 128 : b * 128, :], NT, preferred_element_type=f32
            ).astype(bf16)

        return go

    def score(kb, tile, slot, i):
        h = tile * HEAD_TILE + i
        keys = jnp.concatenate([kn[:, h * 128 : (h + 1) * 128], kr[kb]], axis=1)
        sbuf[slot, i * ROWS : (i + 1) * ROWS, :] = lax.dot_general(
            qx[h * ROWS : (h + 1) * ROWS, :], keys, NT, preferred_element_type=f32
        )

    def weigh(kb, tile, slot, i, fresh):
        r0 = (tile * HEAD_TILE + i) * ROWS
        r1 = r0 + ROWS
        a, b = i * ROWS, (i + 1) * ROWS
        qp = qpos[...]
        s = [
            jnp.where(
                kp[kb, 0:1, c * 128 : (c + 1) * 128] <= qp,
                sbuf[slot, a:b, c * 128 : (c + 1) * 128],
                LOW,
            )
            for c in range(PIECE // 128)
        ]
        top = functools.reduce(jnp.maximum, s)
        top = jnp.max(top, axis=1, keepdims=True)
        if fresh:
            new = jnp.broadcast_to(top, (ROWS, 128))
        else:
            old = mref[r0:r1, :]
            new = jnp.maximum(old, top)
            factor = jnp.exp2((old - new) * SCALE)
        base = new * SCALE
        w = [jnp.exp2(v * SCALE - base) for v in s]
        total = functools.reduce(jnp.add, w)
        mref[r0:r1, :] = new
        lref[r0:r1, :] = total if fresh else lref[r0:r1, :] * factor + total
        wb = jnp.concatenate([v.astype(bf16) for v in w], axis=1)
        product = lax.dot_general(wb, kv[kb], NN, preferred_element_type=f32)
        if fresh:
            acc[r0:r1, :] = product
        else:
            for c in range(LATENT // 128):
                cols = slice(c * 128, (c + 1) * 128)
                acc[r0:r1, cols] = acc[r0:r1, cols] * factor + product[:, cols]

    for n, piece in enumerate(ids):
        rows = pieces[n][...].reshape(PIECE, LATENT + ROPE)
        kv[n] = rows[:, 0:LATENT]
        kr[n] = jnp.concatenate([rows[:, LATENT:], zk], axis=1)
        kp[n, 0:1, :] = kpos[piece : piece + 1, :]

    def block(kb, fresh):
        for t in range(TILES):
            expand(t * HEAD_TILE, (t + 1) * HEAD_TILE)(kb)
            if t == 0:
                for i in range(HEAD_TILE):
                    score(kb, 0, 0, i)
                continue
            for i in range(HEAD_TILE):
                score(kb, t, t % 2, i)
                weigh(kb, t - 1, (t - 1) % 2, i, fresh)
        for i in range(HEAD_TILE):
            weigh(kb, TILES - 1, (TILES - 1) % 2, i, fresh)

    if blocks == 1:
        block(0, first)
    else:
        if first:
            mref[...] = jnp.full_like(mref, LOW)
            lref[...] = jnp.zeros_like(lref)
            acc[...] = jnp.zeros_like(acc)

        def body(kb, carry):
            block(kb, False)
            return carry

        lax.fori_loop(0, blocks, body, 0)
    if last:
        for h in range(HEADS):
            r0 = h * ROWS
            den = jnp.sum(lref[r0 : r0 + ROWS, :], axis=1, keepdims=True)
            latent = (acc[r0 : r0 + ROWS, :] / den).astype(bf16)
            out[:, h * 128 : (h + 1) * 128] = jnp.dot(
                latent, wuv[h], preferred_element_type=f32
            ).astype(bf16)


def attend_call(first, last, ids, qpos, kpos, qx, wuk, pieces, wuv, state):
    vmem = pltpu.VMEM
    f32, bf16 = jnp.float32, jnp.bfloat16
    args = [qpos, kpos, qx, wuk, *pieces]
    if last:
        args.append(wuv)
    alias = {}
    if not first:
        if not last:
            alias = {len(args) + i: i for i in range(3)}
        args.extend(state)
    shapes = [
        jax.ShapeDtypeStruct((HEADS * ROWS, LATENT), f32),
        jax.ShapeDtypeStruct((HEADS * ROWS, 128), f32),
        jax.ShapeDtypeStruct((HEADS * ROWS, 128), f32),
    ]
    n = len(ids)
    scratch = [
        vmem((n, PIECE, LATENT), bf16),
        vmem((n, 8, PIECE), jnp.int32),
        vmem((PIECE, HEADS * 128), bf16),
        vmem((n, PIECE, 128), bf16),
        vmem((2, HEAD_TILE * ROWS, PIECE), f32),
    ]
    out_shape = jax.ShapeDtypeStruct((ROWS, HEADS * 128), bf16) if last else shapes
    spec = pl.BlockSpec(memory_space=vmem)
    keys = n * PIECE
    return pl.pallas_call(
        functools.partial(attend, first, last, ids),
        out_shape=out_shape,
        in_specs=[spec] * len(args),
        out_specs=spec if last else [spec] * 3,
        scratch_shapes=scratch,
        input_output_aliases=alias,
        compiler_params=pltpu.CompilerParams(vmem_limit_bytes=14 << 20),
        cost_estimate=pl.CostEstimate(
            flops=2 * HEADS * ROWS * keys * 1024,
            bytes_accessed=1 << 20,
            transcendentals=HEADS * ROWS * keys,
        ),
    )(*args)


def compute(q_nope, q_rope, kv_latent, half_order, w_uk, w_uv):
    bf16 = jnp.bfloat16
    wuk = w_uk.reshape(HEADS * NOPE, LATENT)
    copies = jnp.broadcast_to(kv_latent[None], (32, *kv_latent.shape))
    plane = lax.all_to_all(copies, ("z", "x"), 0, 0, tiled=True)
    qpos = query_positions(half_order)
    kpos = key_positions(half_order)
    spec = pl.BlockSpec(memory_space=pltpu.VMEM)
    qx = pl.pallas_call(
        pack_queries,
        out_shape=jax.ShapeDtypeStruct((HEADS * ROWS, 256), bf16),
        in_specs=[spec] * 2,
        out_specs=spec,
        compiler_params=pltpu.CompilerParams(vmem_limit_bytes=8 << 20),
        name="pack_queries",
    )(q_nope, q_rope)
    first = ring_step(plane)
    other = exchange(plane)
    second = ring_step(other)
    third = ring_step(first)
    first_other = exchange(first)
    second_other = exchange(second)
    third_other = exchange(third)
    pieces = (plane, other, first, first_other, second, second_other, third, third_other)
    state = None
    for n, ids in enumerate(CALLS):
        state = attend_call(
            n == 0,
            n == len(CALLS) - 1,
            ids,
            qpos,
            kpos,
            qx,
            wuk,
            [pieces[i] for i in ids],
            w_uv,
            state,
        )
    return state


def solution(mesh):
    split = Mesh(mesh.devices.reshape(2, 8, 2, 4, 2), ("yh", "z", "yl", "x", "c"))
    ctx, head = ("yh", "z"), ("yl", "x", "c")
    return jax.shard_map(
        compute,
        mesh=split,
        in_specs=(
            P(ctx, head),
            P(ctx, head),
            P((*ctx, *head), None),
            P(),
            P(head, None, None),
            P(head, None, None),
        ),
        out_specs=P(ctx, head),
        check_vma=False,
    )
```

```python
import functools

import jax
import jax.numpy as jnp
from jax import lax
from jax.experimental import pallas as pl
from jax.experimental.pallas import tpu as pltpu
from jax.sharding import Mesh
from jax.sharding import PartitionSpec as P


HEADS = 8
ROWS = 256
NOPE = 128
LATENT = 512
ROPE = 64
PIECE = 512
SCALE = (NOPE + ROPE) ** -0.5 * 1.4426950408889634
LOW = -1e30
NT = (((1,), (1,)), ((), ()))
NN = (((1,), (0,)), ((), ()))
HEAD_TILE = 4
TILES = HEADS // HEAD_TILE
NY = 4
CALLS = ((0,), (1,), (2,), (3, 4), (5, 6), (7,))


def ring_step(value):
    pairs = [
        (y * 2 + c, ((y + (1 - 2 * c)) % NY) * 2 + c) for y in range(NY) for c in range(2)
    ]
    return lax.ppermute(value, ("yh", "yl", "c"), pairs)


def exchange(value):
    return lax.ppermute(value, "c", [(0, 1), (1, 0)])


def prepare(half_order, qn, qr, weight, qx, wuk, qpos, kpos):
    zeros = jnp.zeros((ROWS, 64), jnp.bfloat16)
    wuk[...] = weight[...]
    for h in range(HEADS):
        rows = slice(h * ROWS, (h + 1) * ROWS)
        qx[rows, 0:128] = qn[:, h * 128 : (h + 1) * 128]
        qx[rows, 128:256] = jnp.concatenate([qr[:, h * 64 : (h + 1) * 64], zeros], axis=1)
    y = lax.axis_index("yh") * 2 + lax.axis_index("yl")
    z, c = lax.axis_index("z"), lax.axis_index("c")
    row = lax.broadcasted_iota(jnp.int32, (128, 128), 0)
    for n in range(2):
        block = half_order[(lax.axis_index("yh") * 8 + z) * 2 + n]
        qpos[n * 128 : (n + 1) * 128, :] = row + block * 128
    lane = lax.broadcasted_iota(jnp.int32, (8, PIECE), 1)
    inner = ((lane >> 4) & 3) * 32 + (lane & 15)
    ahead = 1 - 2 * c
    origins = (
        (y, c),
        (y, 1 - c),
        (y - ahead, c),
        (y + ahead, 1 - c),
        (y - ahead, 1 - c),
        (y + ahead, c),
        (y + 2, c),
        (y + 2, 1 - c),
    )
    for n, (ys, cs) in enumerate(origins):
        ys = ys & 3
        pos = inner + cs * 16
        for k in range(8):
            block = half_order[((ys >> 1) * 8 + k) * 2 + (ys & 1)]
            pos = jnp.where(lane >> 6 == k, pos + block * 128, pos)
        kpos[n : n + 1, :] = pos[0:1]


def attend(first, last, ids, *refs):
    f32, bf16 = jnp.float32, jnp.bfloat16
    refs = list(refs)
    take = lambda n: [refs.pop(0) for _ in range(n)]
    qpos, kpos, qx, wuk = take(4)
    pieces = take(len(ids))
    wuv = take(1)[0] if last else None
    state = None if first else take(3)
    if last:
        out = take(1)[0]
        acc, mref, lref = state
    else:
        acc, mref, lref = take(3)
    kn, kr, sbuf = take(3)
    zk = jnp.zeros((PIECE, 64), bf16)

    def latents():
        parts = [p[:, :, 0:LATENT].reshape(PIECE, LATENT) for p in pieces]
        return parts[0] if len(parts) == 1 else jnp.concatenate(parts, axis=0)

    def expand(tile):
        a, b = tile * HEAD_TILE * 128, (tile + 1) * HEAD_TILE * 128
        for n, p in enumerate(pieces):
            kn[n * PIECE : (n + 1) * PIECE, a:b] = lax.dot_general(
                p[:, :, 0:LATENT].reshape(PIECE, LATENT),
                wuk[a:b, :],
                NT,
                preferred_element_type=f32,
            ).astype(bf16)

    def score(tile, i):
        h = tile * HEAD_TILE + i
        keys = jnp.concatenate([kn[:, h * 128 : (h + 1) * 128], kr[...]], axis=1)
        sbuf[tile % 2, i * ROWS : (i + 1) * ROWS, :] = lax.dot_general(
            qx[h * ROWS : (h + 1) * ROWS, :], keys, NT, preferred_element_type=f32
        )

    def weigh(tile, i):
        r0 = (tile * HEAD_TILE + i) * ROWS
        r1 = r0 + ROWS
        a, b = i * ROWS, (i + 1) * ROWS
        qp = qpos[...]
        s = []
        for n, piece in enumerate(ids):
            for c in range(0, PIECE, 128):
                keep = kpos[piece : piece + 1, c : c + 128] <= qp
                at = n * PIECE + c
                s.append(jnp.where(keep, sbuf[tile % 2, a:b, at : at + 128], LOW))
        top = jnp.max(functools.reduce(jnp.maximum, s), axis=1, keepdims=True)
        if first:
            new = jnp.broadcast_to(top, (ROWS, 128))
        else:
            old = mref[r0:r1, :]
            new = jnp.maximum(old, top)
            factor = jnp.exp2((old - new) * SCALE)
        base = new * SCALE
        w = [jnp.exp2(v * SCALE - base) for v in s]
        total = functools.reduce(jnp.add, w)
        if not first:
            total = lref[r0:r1, :] * factor + total
        wb = jnp.concatenate([v.astype(bf16) for v in w], axis=1)
        product = lax.dot_general(wb, latents(), NN, preferred_element_type=f32)
        if first:
            acc[r0:r1, :] = product
        else:
            product = [
                acc[r0:r1, c : c + 128] * factor + product[:, c : c + 128]
                for c in range(0, LATENT, 128)
            ]
        mref[r0:r1, :] = new
        lref[r0:r1, :] = total
        if not first:
            for n, v in enumerate(product):
                acc[r0:r1, n * 128 : (n + 1) * 128] = v

    def finish(h):
        r0 = h * ROWS
        share = 1.0 / jnp.sum(lref[r0 : r0 + ROWS, :], axis=1, keepdims=True)
        latent = (acc[r0 : r0 + ROWS, :] * share).astype(bf16)
        out[:, h * 128 : (h + 1) * 128] = jnp.dot(
            latent, wuv[h], preferred_element_type=f32
        ).astype(bf16)

    for n, p in enumerate(pieces):
        kr[n * PIECE : (n + 1) * PIECE, :] = jnp.concatenate(
            [p[:, :, LATENT:].reshape(PIECE, ROPE), zk], axis=1
        )
    expand(0)
    for i in range(HEAD_TILE):
        score(0, i)
    for tile in range(TILES):
        if tile + 1 < TILES:
            expand(tile + 1)
        for i in range(HEAD_TILE):
            if tile + 1 < TILES:
                score(tile + 1, i)
            weigh(tile, i)
    if last:
        for h in range(HEADS):
            finish(h)


def attend_call(first, last, ids, qpos, kpos, qx, wuk, pieces, wuv, state):
    vmem = pltpu.VMEM
    f32, bf16 = jnp.float32, jnp.bfloat16
    args = [qpos, kpos, qx, wuk, *pieces]
    if last:
        args.append(wuv)
    alias = {}
    if not first:
        if not last:
            alias = {len(args) + i: i for i in range(3)}
        args.extend(state)
    shapes = [
        jax.ShapeDtypeStruct((HEADS * ROWS, LATENT), f32),
        jax.ShapeDtypeStruct((HEADS * ROWS, 128), f32),
        jax.ShapeDtypeStruct((HEADS * ROWS, 128), f32),
    ]
    keys = len(ids) * PIECE
    scratch = [
        vmem((keys, HEADS * 128), bf16),
        vmem((keys, 128), bf16),
        vmem((2, HEAD_TILE * ROWS, keys), f32),
    ]
    out_shape = jax.ShapeDtypeStruct((ROWS, HEADS * 128), bf16) if last else shapes
    spec = pl.BlockSpec(memory_space=vmem)
    return pl.pallas_call(
        functools.partial(attend, first, last, ids),
        out_shape=out_shape,
        in_specs=[spec] * len(args),
        out_specs=spec if last else [spec] * 3,
        scratch_shapes=scratch,
        input_output_aliases=alias,
        compiler_params=pltpu.CompilerParams(vmem_limit_bytes=14 << 20),
        cost_estimate=pl.CostEstimate(
            flops=2 * HEADS * ROWS * keys * 1024,
            bytes_accessed=1 << 20,
            transcendentals=HEADS * ROWS * keys,
        ),
    )(*args)


def compute(q_nope, q_rope, kv_latent, half_order, w_uk, w_uv):
    copies = jnp.broadcast_to(kv_latent[None], (32, *kv_latent.shape))
    plane = lax.all_to_all(copies, ("z", "x"), 0, 0, tiled=True)
    spec = pl.BlockSpec(memory_space=pltpu.VMEM)
    qx, wuk, qpos, kpos = pl.pallas_call(
        prepare,
        out_shape=[
            jax.ShapeDtypeStruct((HEADS * ROWS, 256), jnp.bfloat16),
            jax.ShapeDtypeStruct((HEADS * NOPE, LATENT), jnp.bfloat16),
            jax.ShapeDtypeStruct((ROWS, 128), jnp.int32),
            jax.ShapeDtypeStruct((8, PIECE), jnp.int32),
        ],
        in_specs=[pl.BlockSpec(memory_space=pltpu.SMEM), spec, spec, spec],
        out_specs=[spec] * 4,
        compiler_params=pltpu.CompilerParams(vmem_limit_bytes=8 << 20),
        name="prepare",
    )(half_order, q_nope, q_rope, w_uk.reshape(HEADS * NOPE, LATENT))
    first = ring_step(plane)
    other = exchange(plane)
    second = ring_step(other)
    third = ring_step(first)
    first_other = exchange(first)
    second_other = exchange(second)
    third_other = exchange(third)
    pieces = (plane, other, first, first_other, second, second_other, third, third_other)
    state = None
    for n, ids in enumerate(CALLS):
        state = attend_call(
            n == 0,
            n == len(CALLS) - 1,
            ids,
            qpos,
            kpos,
            qx,
            wuk,
            [pieces[i] for i in ids],
            w_uv,
            state,
        )
    return state


def solution(mesh):
    split = Mesh(mesh.devices.reshape(2, 8, 2, 4, 2), ("yh", "z", "yl", "x", "c"))
    ctx, head = ("yh", "z"), ("yl", "x", "c")
    return jax.shard_map(
        compute,
        mesh=split,
        in_specs=(
            P(ctx, head),
            P(ctx, head),
            P((*ctx, *head), None),
            P(),
            P(head, None, None),
            P(head, None, None),
        ),
        out_specs=P(ctx, head),
        check_vma=False,
    )
```

```python
import functools

import jax
import jax.numpy as jnp
from jax import lax
from jax.experimental import pallas as pl
from jax.experimental.pallas import tpu as pltpu
from jax.sharding import Mesh
from jax.sharding import PartitionSpec as P


HEADS = 8
ROWS = 256
NOPE = 128
LATENT = 512
ROPE = 64
PIECE = 512
SCALE = (NOPE + ROPE) ** -0.5 * 1.4426950408889634
LOW = -1e30
NT = (((1,), (1,)), ((), ()))
NN = (((1,), (0,)), ((), ()))
HEAD_TILE = 4
TILES = HEADS // HEAD_TILE
NY = 4
CALLS = ((0,), (1,), (2,), (3,), (4,), (5,), (6,), (7,))


def ring_step(value):
    pairs = [
        (y * 2 + c, ((y + (1 - 2 * c)) % NY) * 2 + c) for y in range(NY) for c in range(2)
    ]
    return lax.ppermute(value, ("yh", "yl", "c"), pairs)


def exchange(value):
    return lax.ppermute(value, "c", [(0, 1), (1, 0)])


def spread(kv, copies):
    x = kv[...]
    parts = [x[0:8, 0:LATENT], x[8:16, 0:LATENT], x[0:8, LATENT:], x[8:16, LATENT:]]
    row = jnp.concatenate(parts, axis=1)
    for n in range(32):
        copies[n] = row


def prepare(half_order, qn_hbm, qr_hbm, weight, qx, wuk, qpos, kpos, qn, qr, sems):
    moves = [
        pltpu.make_async_copy(source, target, sems.at[n])
        for n, (source, target) in enumerate(((qn_hbm, qn), (qr_hbm, qr), (weight, wuk)))
    ]
    for move in moves:
        move.start()
    y = lax.axis_index("yh") * 2 + lax.axis_index("yl")
    z, c = lax.axis_index("z"), lax.axis_index("c")
    row = lax.broadcasted_iota(jnp.int32, (128, 128), 0)
    for n in range(2):
        block = half_order[(lax.axis_index("yh") * 8 + z) * 2 + n]
        qpos[n * 128 : (n + 1) * 128, :] = row + block * 128
    lane = lax.broadcasted_iota(jnp.int32, (8, PIECE), 1)
    inner = ((lane >> 3) & 3) * 32 + (lane & 7) + (lane >> 8) * 8
    peer_z = (lane >> 5) & 7
    ahead = 1 - 2 * c
    origins = (
        (y, c),
        (y, 1 - c),
        (y - ahead, c),
        (y + ahead, 1 - c),
        (y - ahead, 1 - c),
        (y + ahead, c),
        (y + 2, c),
        (y + 2, 1 - c),
    )
    for n, (ys, cs) in enumerate(origins):
        ys = ys & 3
        pos = inner + cs * 16
        for k in range(8):
            block = half_order[((ys >> 1) * 8 + k) * 2 + (ys & 1)]
            pos = jnp.where(peer_z == k, pos + block * 128, pos)
        kpos[n : n + 1, :] = pos[0:1]
    for move in moves:
        move.wait()
    zeros = jnp.zeros((ROWS, 64), jnp.bfloat16)
    for h in range(HEADS):
        rows = slice(h * ROWS, (h + 1) * ROWS)
        qx[rows, 0:128] = qn[:, h * 128 : (h + 1) * 128]
        qx[rows, 128:256] = jnp.concatenate([qr[:, h * 64 : (h + 1) * 64], zeros], axis=1)


def attend(first, last, ids, *refs):
    f32, bf16 = jnp.float32, jnp.bfloat16
    refs = list(refs)
    take = lambda n: [refs.pop(0) for _ in range(n)]
    qpos, kpos, qx, wuk = take(4)
    pieces = take(len(ids))
    wuv = take(1)[0] if last else None
    state = None if first else take(3)
    if last:
        out = take(1)[0]
        acc, mref, lref = state
    else:
        acc, mref, lref = take(3)
    kn, kr, sbuf = take(3)
    zk = jnp.zeros((PIECE // 2, 64), bf16)

    def latents(which):
        return jnp.concatenate([p[:, a : a + LATENT] for p in which for a in (0, LATENT)], axis=0)

    def expand(tile):
        a, b = tile * HEAD_TILE * 128, (tile + 1) * HEAD_TILE * 128
        for n, p in enumerate(pieces):
            kn[n * PIECE : (n + 1) * PIECE, a:b] = lax.dot_general(
                latents([p]),
                wuk[a:b, :],
                NT,
                preferred_element_type=f32,
            ).astype(bf16)

    def score(tile, i):
        h = tile * HEAD_TILE + i
        keys = jnp.concatenate([kn[:, h * 128 : (h + 1) * 128], kr[...]], axis=1)
        sbuf[tile % 2, i * ROWS : (i + 1) * ROWS, :] = lax.dot_general(
            qx[h * ROWS : (h + 1) * ROWS, :], keys, NT, preferred_element_type=f32
        )

    def weigh(tile, i):
        r0 = (tile * HEAD_TILE + i) * ROWS
        r1 = r0 + ROWS
        a, b = i * ROWS, (i + 1) * ROWS
        qp = qpos[...]
        s = []
        for n, piece in enumerate(ids):
            for c in range(0, PIECE, 128):
                keep = kpos[piece : piece + 1, c : c + 128] <= qp
                at = n * PIECE + c
                s.append(jnp.where(keep, sbuf[tile % 2, a:b, at : at + 128], LOW))
        top = jnp.max(functools.reduce(jnp.maximum, s), axis=1, keepdims=True)
        if first:
            new = jnp.broadcast_to(top, (ROWS, 128))
        else:
            old = mref[r0:r1, :]
            new = jnp.maximum(old, top)
            factor = jnp.exp2((old - new) * SCALE)
        base = new * SCALE
        w = [jnp.exp2(v * SCALE - base) for v in s]
        total = functools.reduce(jnp.add, w)
        if not first:
            total = lref[r0:r1, :] * factor + total
        wb = jnp.concatenate([v.astype(bf16) for v in w], axis=1)
        product = lax.dot_general(wb, latents(pieces), NN, preferred_element_type=f32)
        if first:
            acc[r0:r1, :] = product
        else:
            product = [
                acc[r0:r1, c : c + 128] * factor + product[:, c : c + 128]
                for c in range(0, LATENT, 128)
            ]
        mref[r0:r1, :] = new
        lref[r0:r1, :] = total
        if not first:
            for n, v in enumerate(product):
                acc[r0:r1, n * 128 : (n + 1) * 128] = v

    def finish(h):
        r0 = h * ROWS
        share = 1.0 / jnp.sum(lref[r0 : r0 + ROWS, :], axis=1, keepdims=True)
        latent = (acc[r0 : r0 + ROWS, :] * share).astype(bf16)
        out[:, h * 128 : (h + 1) * 128] = jnp.dot(
            latent, wuv[h], preferred_element_type=f32
        ).astype(bf16)

    for n, p in enumerate(pieces):
        for k in range(2):
            r0, c0 = n * PIECE + k * PIECE // 2, 2 * LATENT + k * ROPE
            kr[r0 : r0 + PIECE // 2, :] = jnp.concatenate([p[:, c0 : c0 + ROPE], zk], axis=1)
    expand(0)
    for i in range(HEAD_TILE):
        score(0, i)
    for tile in range(TILES):
        if tile + 1 < TILES:
            expand(tile + 1)
        for i in range(HEAD_TILE):
            if tile + 1 < TILES:
                score(tile + 1, i)
            weigh(tile, i)
            if last and tile:
                finish((tile - 1) * HEAD_TILE + i)
    if last:
        for i in range(HEAD_TILE):
            finish((TILES - 1) * HEAD_TILE + i)


def attend_call(first, last, ids, qpos, kpos, qx, wuk, pieces, wuv, state):
    vmem = pltpu.VMEM
    f32, bf16 = jnp.float32, jnp.bfloat16
    args = [qpos, kpos, qx, wuk, *pieces]
    if last:
        args.append(wuv)
    alias = {}
    if not first:
        if not last:
            alias = {len(args) + i: i for i in range(3)}
        args.extend(state)
    shapes = [
        jax.ShapeDtypeStruct((HEADS * ROWS, LATENT), f32),
        jax.ShapeDtypeStruct((HEADS * ROWS, 128), f32),
        jax.ShapeDtypeStruct((HEADS * ROWS, 128), f32),
    ]
    keys = len(ids) * PIECE
    scratch = [
        vmem((keys, HEADS * 128), bf16),
        vmem((keys, 128), bf16),
        vmem((2, HEAD_TILE * ROWS, keys), f32),
    ]
    out_shape = jax.ShapeDtypeStruct((ROWS, HEADS * 128), bf16) if last else shapes
    spec = pl.BlockSpec(memory_space=vmem)
    return pl.pallas_call(
        functools.partial(attend, first, last, ids),
        out_shape=out_shape,
        in_specs=[spec] * len(args),
        out_specs=spec if last else [spec] * 3,
        scratch_shapes=scratch,
        input_output_aliases=alias,
        compiler_params=pltpu.CompilerParams(vmem_limit_bytes=14 << 20),
        cost_estimate=pl.CostEstimate(
            flops=2 * HEADS * ROWS * keys * 1024,
            bytes_accessed=1 << 20,
            transcendentals=HEADS * ROWS * keys,
        ),
    )(*args)


def compute(q_nope, q_rope, kv_latent, half_order, w_uk, w_uv):
    spec = pl.BlockSpec(memory_space=pltpu.VMEM)
    width = 2 * (LATENT + ROPE)
    copies = pl.pallas_call(
        spread,
        out_shape=jax.ShapeDtypeStruct((32, 8, width), jnp.bfloat16),
        in_specs=[spec],
        out_specs=spec,
        compiler_params=pltpu.CompilerParams(vmem_limit_bytes=4 << 20),
        name="spread",
    )(kv_latent)
    plane = lax.all_to_all(copies, ("z", "x"), 0, 0, tiled=True)
    plane = plane.reshape(PIECE // 2, width)
    qx, wuk, qpos, kpos = pl.pallas_call(
        prepare,
        out_shape=[
            jax.ShapeDtypeStruct((HEADS * ROWS, 256), jnp.bfloat16),
            jax.ShapeDtypeStruct((HEADS * NOPE, LATENT), jnp.bfloat16),
            jax.ShapeDtypeStruct((ROWS, 128), jnp.int32),
            jax.ShapeDtypeStruct((8, PIECE), jnp.int32),
        ],
        in_specs=[pl.BlockSpec(memory_space=pltpu.SMEM)]
        + [pl.BlockSpec(memory_space=pltpu.HBM)] * 3,
        out_specs=[spec] * 4,
        scratch_shapes=[
            pltpu.VMEM((ROWS, HEADS * NOPE), jnp.bfloat16),
            pltpu.VMEM((ROWS, HEADS * ROPE), jnp.bfloat16),
            pltpu.SemaphoreType.DMA((3,)),
        ],
        compiler_params=pltpu.CompilerParams(vmem_limit_bytes=8 << 20),
        name="prepare",
    )(half_order, q_nope, q_rope, w_uk.reshape(HEADS * NOPE, LATENT))
    first = ring_step(plane)
    other = exchange(plane)
    second = ring_step(other)
    third = ring_step(first)
    first_other = exchange(first)
    second_other = exchange(second)
    third_other = exchange(third)
    pieces = (plane, other, first, first_other, second, second_other, third, third_other)
    state = None
    for n, ids in enumerate(CALLS):
        state = attend_call(
            n == 0,
            n == len(CALLS) - 1,
            ids,
            qpos,
            kpos,
            qx,
            wuk,
            [pieces[i] for i in ids],
            w_uv,
            state,
        )
    return state


def solution(mesh):
    split = Mesh(mesh.devices.reshape(2, 8, 2, 4, 2), ("yh", "z", "yl", "x", "c"))
    ctx, head = ("yh", "z"), ("yl", "x", "c")
    return jax.shard_map(
        compute,
        mesh=split,
        in_specs=(
            P(ctx, head),
            P(ctx, head),
            P((*ctx, *head), None),
            P(),
            P(head, None, None),
            P(head, None, None),
        ),
        out_specs=P(ctx, head),
        check_vma=False,
    )
```
